32 devices in a mesh: groups: 2 (over x), row: 8 (over z, y), col: 2 (over core).
Axes of the slice: x: 2, y: 2, z: 4, core: 2. Of those that a mesh axis runs over, the one named last changes fastest.
Arguments:
- pair_rep: bfloat16 [160, 80, 128], P(('groups', 'row'), 'col'), parts along dimension 0, as said below
- proj_weight: bfloat16 [128, 512], replicated, may hold values from -0.5 to 0.5
- gate_weight: bfloat16 [128, 128], replicated, may hold values from -0.5 to 0.5
- out_weight: bfloat16 [128, 128], replicated, may hold values from -0.5 to 0.5
Outputs:
- update: bfloat16 [160, 80, 128], P(('groups', 'row'), 'col'), parts along dimension 0
The draws below stay inside these ranges and needn't reach their ends.
There are 2 independent parts, one for each index of `groups`. The reference program is written for one: setup_inputs(seed, part) draws one part's arguments, and reference() takes and returns one part's arrays. A program takes and returns all parts, laid end to end along the dimension named above; an argument that names none is the same for every part. Nothing has to cross between parts.
Inputs may be any that keep to these rules, and one draw needn't show every extreme that they name: `pair_rep`: real-valued pair features; each pair position and each channel carries its own scale factor between 1 and 10.
All inputs are finite; a program needn't handle non-finite values.
Results may differ from the reference program's by a relative error of at most 0.0078.
Values may be sent and summed in bfloat16 or wider, within the bound.
A program may use at most 128 MiB of HBM per device.

```python
import math
import jax
import jax.numpy as jnp
from jax import lax

C = 128
CH = 128
L = 80


def draw_pair_rep(key, part):
    first, second, third = jax.random.split(key, 3)
    position_scale = jnp.exp(jax.random.uniform(second, (L, L, 1), jnp.float32, 0.0, math.log(10.0)))
    channel_scale = jnp.exp(jax.random.uniform(third, (C,), jnp.float32, 0.0, math.log(10.0)))
    base = jax.random.normal(first, (L, L, C), jnp.float32)
    return (base * position_scale * channel_scale).astype(jnp.bfloat16)


def bell_draw(rng, dims, deviation, bound, kind=jnp.bfloat16):
    drawn = jax.random.normal(rng, dims, jnp.float32) * deviation
    return jnp.minimum(jnp.maximum(drawn, -bound), bound).astype(kind)


def setup_inputs(seed: int = 0, part: int = 0) -> dict:
    seeds = jax.random.split(jax.random.key(seed), 5)
    part_keys = jax.random.split(jax.random.fold_in(seeds[4], part), 5)
    pair_rep = draw_pair_rep(jax.random.fold_in(jax.random.fold_in(seeds[4], part), 71), part)
    proj_weight = bell_draw(seeds[1], (C, 4 * CH), C ** -0.5, 0.5)
    gate_weight = bell_draw(seeds[2], (C, C), C ** -0.5, 0.5)
    out_weight = bell_draw(seeds[3], (CH, C), CH ** -0.5, 0.5)
    return dict(pair_rep=pair_rep, proj_weight=proj_weight, gate_weight=gate_weight, out_weight=out_weight)


def layer_norm(values):
    average = lax.optimization_barrier(jnp.mean(values, axis=-1, keepdims=True))
    centered = values - average
    spread = lax.optimization_barrier(jnp.mean(centered * centered, axis=-1, keepdims=True))
    return centered * lax.rsqrt(spread + 1e-05)

def reference(pair_rep, proj_weight, gate_weight, out_weight):
    normed = layer_norm(pair_rep.astype(jnp.float32)).astype(jnp.bfloat16)
    flat_rows = normed.reshape(-1, C)
    projected = jnp.dot(flat_rows, proj_weight, preferred_element_type=jnp.float32)
    left_side = (jax.nn.sigmoid(projected[:, :CH]) * projected[:, CH:2 * CH]).astype(jnp.bfloat16)
    right_side = (jax.nn.sigmoid(projected[:, 2 * CH:3 * CH]) * projected[:, 3 * CH:]).astype(jnp.bfloat16)
    left_side = left_side.reshape(L, L, CH).astype(jnp.float32)
    right_side = right_side.reshape(L, L, CH).astype(jnp.float32)
    combined = jnp.einsum('ikc,jkc->ijc', left_side, right_side)
    tri_normed = layer_norm(combined).astype(jnp.bfloat16).reshape(-1, CH)
    gating = jax.nn.sigmoid(jnp.dot(flat_rows, gate_weight, preferred_element_type=jnp.float32))
    update = jnp.dot(tri_normed, out_weight, preferred_element_type=jnp.float32) * gating
    return update.astype(jnp.bfloat16).reshape(L, L, C)
```

```python
import functools

import jax
import jax.numpy as jnp
from jax import lax
from jax.experimental import pallas as pl
from jax.experimental.pallas import tpu as pltpu
from jax.sharding import PartitionSpec as P

MESH = pl.DeviceIdType.MESH
F32 = jnp.float32
BF16 = jnp.bfloat16


def layer_norm(values):
    average = jnp.mean(values, axis=-1, keepdims=True)
    centered = values - average
    spread = jnp.mean(centered * centered, axis=-1, keepdims=True)
    return centered * lax.rsqrt(spread + 1e-05)


def kernel(
    n, rows, cols, chunks, x_ref, wp_ref, wg_ref, wo_ref, out_ref,
    own, right, left, left32, comb, gate,
    own_send, fwd_send, recv, lsend, lrecv,
):
    hid = wo_ref.shape[0]
    half = n // 2
    deep = n // 2
    span = deep // 2
    row, c = lax.axis_index("row"), lax.axis_index("col")
    z, y = row // 2, row % 2
    has_up, has_down = z < deep - 1, z > 0
    barrier = pltpu.get_barrier_semaphore()

    def greet(r, cc):
        pl.semaphore_signal(barrier, inc=1, device_id={"row": r, "col": cc}, device_id_type=MESH)

    greet(row, 1 - c)
    for cc in range(2):
        greet(2 * z + 1 - y, cc)

    @pl.when(has_up)
    def _():
        for cc in range(2):
            greet(row + 2, cc)

    @pl.when(has_down)
    def _():
        for cc in range(2):
            greet(row - 2, cc)

    normed = layer_norm(x_ref[...].astype(F32)).astype(BF16)
    proj = jnp.dot(normed, wp_ref[:, 2 * hid :], preferred_element_type=F32)
    mine = (jax.nn.sigmoid(proj[:, :hid]) * proj[:, hid:]).astype(BF16)
    own[...] = mine
    dest = z // span
    my_slot = row - dest * half

    @pl.when(dest == c)
    def _():
        right[my_slot, c] = mine

    step = rows * cols // chunks
    greeted = 3 + 2 * has_up.astype(jnp.int32) + 2 * has_down.astype(jnp.int32)
    pl.semaphore_wait(barrier, greeted)

    def own_copy(way, q, r):
        return pltpu.make_async_remote_copy(
            src_ref=own.at[pl.ds(q * step, step)],
            dst_ref=right.at[my_slot, c, pl.ds(q * step, step)],
            send_sem=own_send.at[way, q],
            recv_sem=recv.at[my_slot, c, q],
            device_id={"row": r, "col": dest},
            device_id_type=MESH,
        )

    ways = ((0, has_up, row + 2), (1, has_down, row - 2), (2, None, 2 * z + 1 - y), (3, dest != c, row))
    for q in range(chunks):
        for way, cond, r in ways:
            if cond is None:
                own_copy(way, q, r).start()
            else:
                pl.when(cond)(lambda way=way, q=q, r=r: own_copy(way, q, r).start())

    proj = jnp.dot(normed, wp_ref[:, : 2 * hid], preferred_element_type=F32)
    mine = (jax.nn.sigmoid(proj[:, :hid]) * proj[:, hid:]).astype(BF16)
    left[c] = mine
    left32[c] = mine.astype(F32)
    swap = pltpu.make_async_remote_copy(
        src_ref=left.at[c], dst_ref=left.at[c], send_sem=lsend, recv_sem=lrecv,
        device_id={"row": row, "col": 1 - c}, device_id_type=MESH,
    )
    gate[...] = jax.nn.sigmoid(jnp.dot(normed, wg_ref[...], preferred_element_type=F32))
    swap.start()

    def source(t):
        low = c * span
        inside = low + lax.rem(z - low + t + deep, span)
        return jnp.where(z < low, low + t, jnp.where(z >= low + span, low + span - 1 - t, inside))

    def block(slot, kc, q, way, r):
        part = right.at[slot, kc, pl.ds(q * step, step)]
        return pltpu.make_async_remote_copy(
            src_ref=part, dst_ref=part, send_sem=fwd_send.at[slot, kc, q, way],
            recv_sem=recv.at[slot, kc, q], device_id={"row": r, "col": c}, device_id_type=MESH,
        )

    def forwards(t, act):
        zs = source(t)
        slot = zs * 2 + y - c * half

        @pl.when(zs != z)
        def _():
            for q in range(chunks):
                for kc in range(2):
                    act(zs, slot, kc, q)

    def send_on(zs, slot, kc, q):
        block(slot, kc, q, 0, row).wait_recv()

        @pl.when((zs < z) & has_up)
        def _():
            block(slot, kc, q, 0, row + 2).start()

        @pl.when((zs > z) & has_down)
        def _():
            block(slot, kc, q, 0, row - 2).start()

        block(slot, kc, q, 1, 2 * z + 1 - y).start()

    def sent(zs, slot, kc, q):
        @pl.when(((zs < z) & has_up) | ((zs > z) & has_down))
        def _():
            block(slot, kc, q, 0, row).wait_send()

        block(slot, kc, q, 1, row).wait_send()

    def compute(slot):
        @pl.loop(0, rows // 2)
        def _(pair):
            acc = [[None, None] for _ in range(rows)]
            for kc in range(2):
                wide = right[slot, kc, pl.ds(pair * 2 * cols, 2 * cols), :].astype(F32)
                for kt in range(0, cols, 8):
                    r = [wide[j * cols + kt : j * cols + kt + 8] for j in range(2)]
                    for i in range(rows):
                        l = left32[kc, i * cols + kt : i * cols + kt + 8, :]
                        for j in range(2):
                            term = l * r[j]
                            acc[i][j] = term if acc[i][j] is None else acc[i][j] + term
            for i in range(rows):
                for j in range(2):
                    comb[pl.ds(i * cols + slot * rows + pair * 2 + j, 1), :] = jnp.sum(
                        acc[i][j], axis=0, keepdims=True
                    )

    def compute_own(t):
        zs = source(t)

        @pl.when(zs == z)
        def _():
            for q in range(chunks):
                block(zs * 2 + y - c * half, 1 - c, q, 0, row).wait_recv()

        compute(zs * 2 + y - c * half)

    def compute_other(t):
        slot = source(t) * 2 + 1 - y - c * half
        for q in range(chunks):
            for kc in range(2):
                block(slot, kc, q, 0, row).wait_recv()
        compute(slot)

    forwards(0, send_on)
    pltpu.make_async_remote_copy(
        src_ref=left.at[1 - c], dst_ref=left.at[1 - c], send_sem=lsend, recv_sem=lrecv,
        device_id={"row": row, "col": 1 - c}, device_id_type=MESH,
    ).wait_recv()
    left32[1 - c] = left[1 - c].astype(F32)
    compute_own(0)

    @pl.loop(1, span)
    def _(t):
        forwards(t, send_on)
        compute_other(t - 1)
        compute_own(t)

    compute_other(span - 1)

    tri = layer_norm(comb[...]).astype(BF16)
    update = jnp.dot(tri, wo_ref[...], preferred_element_type=F32) * gate[...]
    out_ref[...] = update.astype(BF16)

    for q in range(chunks):
        for way, cond, r in ways:
            if cond is None:
                own_copy(way, q, r).wait_send()
            else:
                pl.when(cond)(lambda way=way, q=q, r=r: own_copy(way, q, r).wait_send())
    swap.wait_send()

    @pl.loop(0, span)
    def _(t):
        forwards(t, sent)


def per_device(n, pair_rep, proj_weight, gate_weight, out_weight):
    rows, cols, channels = pair_rep.shape
    hid = out_weight.shape[0]
    flat = rows * cols
    chunks = rows // 2
    vmem = pl.BlockSpec(memory_space=pltpu.VMEM)
    dma = pltpu.SemaphoreType.DMA
    out = pl.pallas_call(
        functools.partial(kernel, n, rows, cols, chunks),
        out_shape=jax.ShapeDtypeStruct((flat, channels), BF16),
        in_specs=[vmem] * 4,
        out_specs=vmem,
        scratch_shapes=[
            pltpu.VMEM((flat, hid), BF16),
            pltpu.VMEM((n // 2, 2, flat, hid), BF16),
            pltpu.VMEM((2, flat, hid), BF16),
            pltpu.VMEM((2, flat, hid), F32),
            pltpu.VMEM((flat, hid), F32),
            pltpu.VMEM((flat, channels), F32),
            dma((4, chunks)),
            dma((n // 2, 2, chunks, 2)),
            dma((n // 2, 2, chunks)),
            dma,
            dma,
        ],
        compiler_params=pltpu.CompilerParams(
            collective_id=0, has_side_effects=True, vmem_limit_bytes=60 * 1024 * 1024
        ),
    )(pair_rep.reshape(flat, channels), proj_weight, gate_weight, out_weight)
    return out.reshape(rows, cols, channels)


def solution(mesh):
    placed = (P(("groups", "row"), "col", None), P(), P(), P())
    return jax.shard_map(
        functools.partial(per_device, mesh.shape["row"]),
        mesh=mesh,
        in_specs=placed,
        out_specs=P(("groups", "row"), "col", None),
        check_vma=False,
    )
```

```python
import functools

import jax
import jax.numpy as jnp
from jax import lax
from jax.experimental import pallas as pl
from jax.experimental.pallas import tpu as pltpu
from jax.sharding import PartitionSpec as P

MESH = pl.DeviceIdType.MESH
F32 = jnp.float32
BF16 = jnp.bfloat16


def layer_norm(values):
    average = jnp.mean(values, axis=-1, keepdims=True)
    centered = values - average
    spread = jnp.mean(centered * centered, axis=-1, keepdims=True)
    return centered * lax.rsqrt(spread + 1e-05)


def kernel(
    n, rows, cols, chunks, x_ref, wp_ref, wg_ref, wo_ref, out_ref,
    own, right, left, left32, comb, gate, stage, back,
    own_send, fwd_send, recv, lsend, lrecv, ret_send, ret_recv,
):
    hid = wo_ref.shape[0]
    deep = n // 2
    span = deep // 2
    row, c = lax.axis_index("row"), lax.axis_index("col")
    z, y = row // 2, row % 2
    across = 2 * z + 1 - y
    has_up, has_down = z < deep - 1, z > 0
    low = c * span
    barrier = pltpu.get_barrier_semaphore()

    def greet(r, cc):
        pl.semaphore_signal(barrier, inc=1, device_id={"row": r, "col": cc}, device_id_type=MESH)

    greet(row, 1 - c)
    greet(across, c)

    @pl.when(has_up)
    def _():
        for cc in range(2):
            greet(row + 2, cc)

    @pl.when(has_down)
    def _():
        for cc in range(2):
            greet(row - 2, cc)

    normed = layer_norm(x_ref[...].astype(F32)).astype(BF16)
    proj = jnp.dot(normed, wp_ref[:, 2 * hid :], preferred_element_type=F32)
    mine = (jax.nn.sigmoid(proj[:, :hid]) * proj[:, hid:]).astype(BF16)
    own[...] = mine
    dest = z // span
    my_slot = z - dest * span

    @pl.when(dest == c)
    def _():
        right[my_slot, c] = mine

    step = rows * cols // chunks
    greeted = 2 + 2 * has_up.astype(jnp.int32) + 2 * has_down.astype(jnp.int32)
    pl.semaphore_wait(barrier, greeted)

    def own_copy(way, q, r):
        return pltpu.make_async_remote_copy(
            src_ref=own.at[pl.ds(q * step, step)],
            dst_ref=right.at[my_slot, c, pl.ds(q * step, step)],
            send_sem=own_send.at[way, q],
            recv_sem=recv.at[my_slot, c, q],
            device_id={"row": r, "col": dest},
            device_id_type=MESH,
        )

    ways = ((0, has_up, row + 2), (1, has_down, row - 2), (2, dest != c, row))
    for q in range(chunks):
        for way, cond, r in ways:
            pl.when(cond)(lambda way=way, q=q, r=r: own_copy(way, q, r).start())

    def left_copy(which, kc, way, r, cc):
        part = left.at[which, kc]
        return pltpu.make_async_remote_copy(
            src_ref=part, dst_ref=part, send_sem=lsend.at[way], recv_sem=lrecv.at[which, kc],
            device_id={"row": r, "col": cc}, device_id_type=MESH,
        )

    proj = jnp.dot(normed, wp_ref[:, : 2 * hid], preferred_element_type=F32)
    mine = (jax.nn.sigmoid(proj[:, :hid]) * proj[:, hid:]).astype(BF16)
    left[y, c] = mine
    left32[y, c] = mine.astype(F32)
    gate[...] = jax.nn.sigmoid(jnp.dot(normed, wg_ref[...], preferred_element_type=F32))
    left_copy(y, c, 0, across, c).start()
    left_copy(y, c, 1, row, 1 - c).start()

    def source(t):
        inside = low + lax.rem(z - low + t + 1 + deep, span)
        return jnp.where(z < low, low + t, jnp.where(z >= low + span, low + span - 1 - t, inside))

    def passes(zs):
        return ((zs < z) & has_up) | ((zs > z) & has_down)

    def block(slot, kc, q, r):
        part = right.at[slot, kc, pl.ds(q * step, step)]
        return pltpu.make_async_remote_copy(
            src_ref=part, dst_ref=part, send_sem=fwd_send.at[slot, kc, q],
            recv_sem=recv.at[slot, kc, q], device_id={"row": r, "col": c}, device_id_type=MESH,
        )

    def send_on(t, q):
        zs = source(t)

        @pl.when(passes(zs))
        def _():
            for kc in range(2):
                block(zs - low, kc, q, row).wait_recv()
                block(zs - low, kc, q, jnp.where(zs < z, row + 2, row - 2)).start()

    early = chunks - 2
    for q in range(early):
        send_on(0, q)
    left_copy(1 - y, c, 2, row, 1 - c).wait_recv()
    left_copy(1 - y, c, 2, row, 1 - c).start()
    for q in range(early, chunks):
        send_on(0, q)

    @pl.loop(1, span)
    def _(t):
        for q in range(chunks):
            send_on(t, q)

    left32[1 - y, c] = left[1 - y, c].astype(F32)
    for which in (y, 1 - y):
        left_copy(which, 1 - c, 0, row, c).wait_recv()
        left32[which, 1 - c] = left[which, 1 - c].astype(F32)

    def ret_copy(slot, pair):
        return pltpu.make_async_remote_copy(
            src_ref=stage.at[slot, pair], dst_ref=back.at[slot, pair],
            send_sem=ret_send.at[slot, pair], recv_sem=ret_recv.at[slot, pair],
            device_id={"row": across, "col": c}, device_id_type=MESH,
        )

    def sums(which, slot, pair, put):
        acc = [[None, None] for _ in range(rows)]
        for kc in range(2):
            wide = right[slot, kc, pl.ds(pair * 2 * cols, 2 * cols), :].astype(F32)
            for kt in range(0, cols, 8):
                r = [wide[j * cols + kt : j * cols + kt + 8] for j in range(2)]
                for i in range(rows):
                    l = left32[which, kc, i * cols + kt : i * cols + kt + 8, :]
                    for j in range(2):
                        term = l * r[j]
                        acc[i][j] = term if acc[i][j] is None else acc[i][j] + term
        for i in range(rows):
            for j in range(2):
                put(i, j, jnp.sum(acc[i][j], axis=0, keepdims=True))

    def place(i, j, slot, pair, side, value):
        comb[pl.ds(i * cols + (slot * 2 + side) * rows + pair * 2 + j, 1), :] = value

    @pl.loop(0, span)
    def _(t):
        zs = source(lax.rem(t + jnp.where((z >= low) & (z < low + span), span - 1, 0), span))
        slot = zs - low

        @pl.loop(0, chunks)
        def _(pair):
            for kc in range(2):
                @pl.when(jnp.logical_not(passes(zs)) & ((zs != z) | (c != kc)))
                def _(kc=kc):
                    block(slot, kc, pair, row).wait_recv()

            def put_stage(i, j, value):
                stage[slot, pair, j * rows + i : j * rows + i + 1, :] = value

            sums(1 - y, slot, pair, put_stage)
            sums(y, slot, pair, lambda i, j, value: place(i, j, slot, pair, y, value))
            ret_copy(slot, pair).start()

    @pl.loop(0, span)
    def _(t):
        slot = source(lax.rem(t + jnp.where((z >= low) & (z < low + span), span - 1, 0), span)) - low

        @pl.loop(0, chunks)
        def _(pair):
            ret_copy(slot, pair).wait_recv()
            for i in range(rows):
                for j in range(2):
                    got = back[slot, pair, j * rows + i : j * rows + i + 1, :]
                    place(i, j, slot, pair, 1 - y, got)

    tri = layer_norm(comb[...]).astype(BF16)
    update = jnp.dot(tri, wo_ref[...], preferred_element_type=F32) * gate[...]
    out_ref[...] = update.astype(BF16)

    for q in range(chunks):
        for way, cond, r in ways:
            pl.when(cond)(lambda way=way, q=q, r=r: own_copy(way, q, r).wait_send())
    left_copy(y, c, 0, across, c).wait_send()
    left_copy(y, c, 1, row, 1 - c).wait_send()
    left_copy(1 - y, c, 2, row, 1 - c).wait_send()

    @pl.loop(0, span)
    def _(slot):
        @pl.when(passes(slot + low))
        def _():
            for q in range(chunks):
                for kc in range(2):
                    block(slot, kc, q, row).wait_send()

        for q in range(chunks):
            ret_copy(slot, q).wait_send()


def per_device(n, pair_rep, proj_weight, gate_weight, out_weight):
    rows, cols, channels = pair_rep.shape
    hid = out_weight.shape[0]
    flat = rows * cols
    chunks = rows // 2
    span = n // 4
    padded = -(-2 * rows // 8) * 8
    vmem = pl.BlockSpec(memory_space=pltpu.VMEM)
    dma = pltpu.SemaphoreType.DMA
    out = pl.pallas_call(
        functools.partial(kernel, n, rows, cols, chunks),
        out_shape=jax.ShapeDtypeStruct((flat, channels), BF16),
        in_specs=[vmem] * 4,
        out_specs=vmem,
        scratch_shapes=[
            pltpu.VMEM((flat, hid), BF16),
            pltpu.VMEM((span, 2, flat, hid), BF16),
            pltpu.VMEM((2, 2, flat, hid), BF16),
            pltpu.VMEM((2, 2, flat, hid), F32),
            pltpu.VMEM((flat, hid), F32),
            pltpu.VMEM((flat, channels), F32),
            pltpu.VMEM((span, chunks, padded, hid), F32),
            pltpu.VMEM((span, chunks, padded, hid), F32),
            dma((3, chunks)),
            dma((span, 2, chunks)),
            dma((span, 2, chunks)),
            dma((3,)),
            dma((2, 2)),
            dma((span, chunks)),
            dma((span, chunks)),
        ],
        compiler_params=pltpu.CompilerParams(
            collective_id=0, has_side_effects=True, vmem_limit_bytes=60 * 1024 * 1024
        ),
    )(pair_rep.reshape(flat, channels), proj_weight, gate_weight, out_weight)
    return out.reshape(rows, cols, channels)


def solution(mesh):
    placed = (P(("groups", "row"), "col", None), P(), P(), P())
    return jax.shard_map(
        functools.partial(per_device, mesh.shape["row"]),
        mesh=mesh,
        in_specs=placed,
        out_specs=P(("groups", "row"), "col", None),
        check_vma=False,
    )
```

```python
import functools

import jax
import jax.numpy as jnp
from jax import lax
from jax.experimental import pallas as pl
from jax.experimental.pallas import tpu as pltpu
from jax.sharding import PartitionSpec as P

MESH = pl.DeviceIdType.MESH
F32 = jnp.float32
BF16 = jnp.bfloat16


def layer_norm(values):
    average = jnp.mean(values, axis=-1, keepdims=True)
    centered = values - average
    spread = jnp.mean(centered * centered, axis=-1, keepdims=True)
    return centered * lax.rsqrt(spread + 1e-05)


def kernel(
    n, rows, cols, pairs, sub, x_hbm, wp_hbm, wg_hbm, wo_hbm, out_ref,
    x_ref, wp_ref, wg_ref, wo_ref, normed, in_sem, own, right, left, left32, comb, gate, stage, back,
    own_send, fwd_send, recv, lsend, lrecv, ret_send, ret_recv,
):
    hid = wo_ref.shape[0]
    chunks = pairs * sub
    flat = rows * cols
    part = flat // pairs
    loads = [pltpu.make_async_copy(x_hbm, x_ref, in_sem.at[0])]
    for k in (1, 0):
        cut = (slice(None), pl.ds(2 * hid * k, 2 * hid))
        loads.append(pltpu.make_async_copy(wp_hbm.at[cut], wp_ref.at[k], in_sem.at[len(loads)]))
    loads.append(pltpu.make_async_copy(wg_hbm, wg_ref, in_sem.at[3]))
    loads.append(pltpu.make_async_copy(wo_hbm, wo_ref, in_sem.at[4]))
    for load in loads:
        load.start()
    deep = n // 2
    span = deep // 2
    row, c = lax.axis_index("row"), lax.axis_index("col")
    z, y = row // 2, row % 2
    across = 2 * z + 1 - y
    has_up, has_down = z < deep - 1, z > 0
    low = c * span
    barrier = pltpu.get_barrier_semaphore()

    def greet(r, cc):
        pl.semaphore_signal(barrier, inc=1, device_id={"row": r, "col": cc}, device_id_type=MESH)

    greet(row, 1 - c)
    greet(across, c)

    @pl.when(has_up)
    def _():
        for cc in range(2):
            greet(row + 2, cc)

    @pl.when(has_down)
    def _():
        for cc in range(2):
            greet(row - 2, cc)

    dest = z // span
    my_slot = z - dest * span
    step = flat // chunks

    def gated(values, k):
        proj = jnp.dot(values, wp_ref[k], preferred_element_type=F32)
        return (jax.nn.sigmoid(proj[:, :hid]) * proj[:, hid:]).astype(BF16)

    def prepare(p):
        here = pl.ds(p * part, part)
        values = layer_norm(x_ref[here, :].astype(F32)).astype(BF16)
        normed[here, :] = values
        own[here, :] = gated(values, 1)

    loads[0].wait()
    loads[1].wait()

    def own_copy(way, q, r):
        return pltpu.make_async_remote_copy(
            src_ref=own.at[pl.ds(q * step, step)],
            dst_ref=right.at[my_slot, c, pl.ds(q * step, step)],
            send_sem=own_send.at[way, q],
            recv_sem=recv.at[my_slot, c, q],
            device_id={"row": r, "col": dest},
            device_id_type=MESH,
        )

    ways = ((0, has_down, row - 2), (1, has_up, row + 2), (2, dest != c, row))

    def own_all(p, act):
        for way, cond, r in ways:
            @pl.when(cond)
            def _(way=way, r=r):
                for q in range(p * sub, (p + 1) * sub):
                    act(own_copy(way, q, r))

    prepare(0)
    greeted = 2 + 2 * has_up.astype(jnp.int32) + 2 * has_down.astype(jnp.int32)
    pl.semaphore_wait(barrier, greeted)
    for p in range(1, pairs):
        prepare(p)
        own_all(p - 1, lambda copy: copy.start())
    own_all(pairs - 1, lambda copy: copy.start())

    @pl.when(dest == c)
    def _():
        right[my_slot, c] = own[...]

    def left_copy(which, kc, way, r, cc):
        part = left.at[which, kc]
        return pltpu.make_async_remote_copy(
            src_ref=part, dst_ref=part, send_sem=lsend.at[way], recv_sem=lrecv.at[which, kc],
            device_id={"row": r, "col": cc}, device_id_type=MESH,
        )

    loads[2].wait()
    loads[3].wait()
    mine = gated(normed[...], 0)
    left[y, c] = mine
    left32[y, c] = mine.astype(F32)
    gate[...] = jax.nn.sigmoid(jnp.dot(normed[...], wg_ref[...], preferred_element_type=F32))
    left_copy(y, c, 0, across, c).start()
    left_copy(y, c, 1, row, 1 - c).start()

    def source(t):
        inside = low + lax.rem(z - low + t + 1 + deep, span)
        return jnp.where(z < low, low + t, jnp.where(z >= low + span, low + span - 1 - t, inside))

    def passes(zs):
        return ((zs < z) & has_up) | ((zs > z) & has_down)

    def block(slot, kc, q, r):
        part = right.at[slot, kc, pl.ds(q * step, step)]
        return pltpu.make_async_remote_copy(
            src_ref=part, dst_ref=part, send_sem=fwd_send.at[slot, kc, q],
            recv_sem=recv.at[slot, kc, q], device_id={"row": r, "col": c}, device_id_type=MESH,
        )

    def send_on(t, q):
        zs = source(t)

        @pl.when(passes(zs))
        def _():
            for kc in range(2):
                block(zs - low, kc, q, row).wait_recv()
                block(zs - low, kc, q, jnp.where(zs < z, row + 2, row - 2)).start()

    early = chunks - 2 * sub
    pl.loop(0, early)(lambda q: send_on(0, q))
    left_copy(1 - y, c, 2, row, 1 - c).wait_recv()
    left_copy(1 - y, c, 2, row, 1 - c).start()
    pl.loop(early, chunks)(lambda q: send_on(0, q))

    @pl.loop(1, span)
    def _(t):
        pl.loop(0, chunks)(lambda q: send_on(t, q))

    left32[1 - y, c] = left[1 - y, c].astype(F32)
    for which in (y, 1 - y):
        left_copy(which, 1 - c, 0, row, c).wait_recv()
        left32[which, 1 - c] = left[which, 1 - c].astype(F32)

    def ret_copy(slot, pair):
        return pltpu.make_async_remote_copy(
            src_ref=stage.at[slot, pair], dst_ref=back.at[slot, pair],
            send_sem=ret_send.at[slot, pair], recv_sem=ret_recv.at[slot, pair],
            device_id={"row": across, "col": c}, device_id_type=MESH,
        )

    def sums(which, slot, pair, put):
        acc = [[None, None] for _ in range(rows)]
        for kc in range(2):
            wide = right[slot, kc, pl.ds(pair * 2 * cols, 2 * cols), :].astype(F32)
            for kt in range(0, cols, 8):
                r = [wide[j * cols + kt : j * cols + kt + 8] for j in range(2)]
                for i in range(rows):
                    l = left32[which, kc, i * cols + kt : i * cols + kt + 8, :]
                    for j in range(2):
                        term = l * r[j]
                        acc[i][j] = term if acc[i][j] is None else acc[i][j] + term
        for i in range(rows):
            for j in range(2):
                put(i, j, jnp.sum(acc[i][j], axis=0, keepdims=True))

    def place(i, j, slot, pair, side, value):
        comb[pl.ds(i * cols + (slot * 2 + side) * rows + pair * 2 + j, 1), :] = value

    @pl.loop(0, span)
    def _(t):
        zs = source(lax.rem(t + jnp.where((z >= low) & (z < low + span), span - 1, 0), span))
        slot = zs - low

        @pl.loop(0, pairs)
        def _(pair):
            for kc in range(2):
                @pl.when(jnp.logical_not(passes(zs)) & ((zs != z) | (c != kc)))
                def _(kc=kc):
                    for q in range(sub):
                        block(slot, kc, pair * sub + q, row).wait_recv()

            def put_stage(i, j, value):
                stage[slot, pair, j * rows + i : j * rows + i + 1, :] = value

            sums(1 - y, slot, pair, put_stage)
            sums(y, slot, pair, lambda i, j, value: place(i, j, slot, pair, y, value))
            ret_copy(slot, pair).start()

    @pl.loop(0, span)
    def _(t):
        slot = source(lax.rem(t + jnp.where((z >= low) & (z < low + span), span - 1, 0), span)) - low

        @pl.loop(0, pairs)
        def _(pair):
            ret_copy(slot, pair).wait_recv()
            for i in range(rows):
                for j in range(2):
                    got = back[slot, pair, j * rows + i : j * rows + i + 1, :]
                    place(i, j, slot, pair, 1 - y, got)

    loads[4].wait()
    tri = layer_norm(comb[...]).astype(BF16)
    update = jnp.dot(tri, wo_ref[...], preferred_element_type=F32) * gate[...]
    out_ref[...] = update.astype(BF16)

    for p in range(pairs):
        own_all(p, lambda copy: copy.wait_send())
    left_copy(y, c, 0, across, c).wait_send()
    left_copy(y, c, 1, row, 1 - c).wait_send()
    left_copy(1 - y, c, 2, row, 1 - c).wait_send()

    @pl.loop(0, span)
    def _(slot):
        @pl.when(passes(slot + low))
        def _():
            @pl.loop(0, chunks)
            def _(q):
                for kc in range(2):
                    block(slot, kc, q, row).wait_send()

        for pair in range(pairs):
            ret_copy(slot, pair).wait_send()


def per_device(n, pair_rep, proj_weight, gate_weight, out_weight):
    rows, cols, channels = pair_rep.shape
    hid = out_weight.shape[0]
    flat = rows * cols
    pairs = rows // 2
    sub = 1
    chunks = pairs * sub
    span = n // 4
    padded = -(-2 * rows // 8) * 8
    vmem = pl.BlockSpec(memory_space=pltpu.VMEM)
    dma = pltpu.SemaphoreType.DMA
    out = pl.pallas_call(
        functools.partial(kernel, n, rows, cols, pairs, sub),
        out_shape=pltpu.VMEM((flat, channels), BF16),
        in_specs=[pl.BlockSpec(memory_space=pl.ANY)] * 4,
        out_specs=vmem,
        scratch_shapes=[
            pltpu.VMEM((flat, channels), BF16),
            pltpu.VMEM((2, channels, 2 * hid), BF16),
            pltpu.VMEM((channels, channels), BF16),
            pltpu.VMEM((hid, channels), BF16),
            pltpu.VMEM((flat, channels), BF16),
            dma((5,)),
            pltpu.VMEM((flat, hid), BF16),
            pltpu.VMEM((span, 2, flat, hid), BF16),
            pltpu.VMEM((2, 2, flat, hid), BF16),
            pltpu.VMEM((2, 2, flat, hid), F32),
            pltpu.VMEM((flat, hid), F32),
            pltpu.VMEM((flat, channels), F32),
            pltpu.VMEM((span, pairs, padded, hid), F32),
            pltpu.VMEM((span, pairs, padded, hid), F32),
            dma((3, chunks)),
            dma((span, 2, chunks)),
            dma((span, 2, chunks)),
            dma((3,)),
            dma((2, 2)),
            dma((span, pairs)),
            dma((span, pairs)),
        ],
        compiler_params=pltpu.CompilerParams(
            collective_id=0, has_side_effects=True, vmem_limit_bytes=60 * 1024 * 1024
        ),
    )(pair_rep.reshape(flat, channels), proj_weight, gate_weight, out_weight)
    return out.reshape(rows, cols, channels)


def solution(mesh):
    placed = (P(("groups", "row"), "col", None), P(), P(), P())
    return jax.shard_map(
        functools.partial(per_device, mesh.shape["row"]),
        mesh=mesh,
        in_specs=placed,
        out_specs=P(("groups", "row"), "col", None),
        check_vma=False,
    )
```

```python
import functools

import jax
import jax.numpy as jnp
from jax import lax
from jax.experimental import pallas as pl
from jax.experimental.pallas import tpu as pltpu
from jax.sharding import PartitionSpec as P

MESH = pl.DeviceIdType.MESH
F32 = jnp.float32
BF16 = jnp.bfloat16


def layer_norm(values):
    average = jnp.mean(values, axis=-1, keepdims=True)
    centered = values - average
    spread = jnp.mean(centered * centered, axis=-1, keepdims=True)
    return centered * lax.rsqrt(spread + 1e-05)


def kernel(
    n, rows, cols, pairs, sub, x_hbm, wp_hbm, wg_hbm, wo_hbm, out_ref,
    x_ref, wp_ref, wg_ref, wo_ref, normed, in_sem, x_sem, own, right, left, left32, comb, gate, stage, back,
    own_send, fwd_send, recv, lsend, lrecv, ret_send, ret_recv,
):
    hid = wo_ref.shape[0]
    chunks = pairs * sub
    flat = rows * cols
    part = flat // pairs
    x_loads = [
        pltpu.make_async_copy(x_hbm.at[pl.ds(p * part, part)], x_ref.at[pl.ds(p * part, part)], x_sem.at[p])
        for p in range(pairs)
    ]
    loads = []
    for k in (1, 0):
        cut = (slice(None), pl.ds(2 * hid * k, 2 * hid))
        loads.append(pltpu.make_async_copy(wp_hbm.at[cut], wp_ref.at[k], in_sem.at[len(loads)]))
    loads.append(pltpu.make_async_copy(wg_hbm, wg_ref, in_sem.at[2]))
    loads.append(pltpu.make_async_copy(wo_hbm, wo_ref, in_sem.at[3]))
    for load in [x_loads[0], loads[0]] + x_loads[1:] + loads[1:]:
        load.start()
    deep = n // 2
    span = deep // 2
    row, c = lax.axis_index("row"), lax.axis_index("col")
    z, y = row // 2, row % 2
    across = 2 * z + 1 - y
    has_up, has_down = z < deep - 1, z > 0
    low = c * span
    barrier = pltpu.get_barrier_semaphore()

    def greet(r, cc):
        pl.semaphore_signal(barrier, inc=1, device_id={"row": r, "col": cc}, device_id_type=MESH)

    greet(row, 1 - c)
    greet(across, c)

    @pl.when(has_up)
    def _():
        for cc in range(2):
            greet(row + 2, cc)

    @pl.when(has_down)
    def _():
        for cc in range(2):
            greet(row - 2, cc)

    dest = z // span
    my_slot = z - dest * span
    step = flat // chunks

    def gated(values, k):
        proj = jnp.dot(values, wp_ref[k], preferred_element_type=F32)
        return (jax.nn.sigmoid(proj[:, :hid]) * proj[:, hid:]).astype(BF16)

    def prepare(p):
        x_loads[p].wait()
        here = pl.ds(p * part, part)
        values = layer_norm(x_ref[here, :].astype(F32)).astype(BF16)
        normed[here, :] = values
        own[here, :] = gated(values, 1)

    loads[0].wait()

    def own_copy(way, q, r):
        return pltpu.make_async_remote_copy(
            src_ref=own.at[pl.ds(q * step, step)],
            dst_ref=right.at[my_slot, c, pl.ds(q * step, step)],
            send_sem=own_send.at[way, q],
            recv_sem=recv.at[my_slot, c, q],
            device_id={"row": r, "col": dest},
            device_id_type=MESH,
        )

    ways = ((0, has_down, row - 2), (1, has_up, row + 2), (2, dest != c, row))

    def own_all(p, act):
        for way, cond, r in ways:
            @pl.when(cond)
            def _(way=way, r=r):
                for q in range(p * sub, (p + 1) * sub):
                    act(own_copy(way, q, r))

    prepare(0)
    greeted = 2 + 2 * has_up.astype(jnp.int32) + 2 * has_down.astype(jnp.int32)
    pl.semaphore_wait(barrier, greeted)
    own_all(0, lambda copy: copy.start())
    for p in range(1, pairs):
        prepare(p)
        if p > 1:
            own_all(p - 1, lambda copy: copy.start())
    own_all(pairs - 1, lambda copy: copy.start())

    @pl.when(dest == c)
    def _():
        right[my_slot, c] = own[...]

    def left_copy(which, kc, way, r, cc):
        part = left.at[which, kc]
        return pltpu.make_async_remote_copy(
            src_ref=part, dst_ref=part, send_sem=lsend.at[way], recv_sem=lrecv.at[which, kc],
            device_id={"row": r, "col": cc}, device_id_type=MESH,
        )

    loads[1].wait()
    loads[2].wait()
    mine = gated(normed[...], 0)
    left[y, c] = mine
    left32[y, c] = mine.astype(F32)
    left_copy(y, c, 0, across, c).start()
    left_copy(y, c, 1, row, 1 - c).start()

    def source(t):
        inside = low + lax.rem(z - low + t + 1 + deep, span)
        return jnp.where(z < low, low + t, jnp.where(z >= low + span, low + span - 1 - t, inside))

    def passes(zs):
        return ((zs < z) & has_up) | ((zs > z) & has_down)

    def block(slot, kc, q, r):
        part = right.at[slot, kc, pl.ds(q * step, step)]
        return pltpu.make_async_remote_copy(
            src_ref=part, dst_ref=part, send_sem=fwd_send.at[slot, kc, q],
            recv_sem=recv.at[slot, kc, q], device_id={"row": r, "col": c}, device_id_type=MESH,
        )

    def send_on(t, q):
        zs = source(t)

        @pl.when(passes(zs))
        def _():
            for kc in range(2):
                block(zs - low, kc, q, row).wait_recv()
                block(zs - low, kc, q, jnp.where(zs < z, row + 2, row - 2)).start()

    early = chunks - sub
    pl.loop(0, early)(lambda q: send_on(0, q))
    left_copy(1 - y, c, 2, row, 1 - c).wait_recv()
    left_copy(1 - y, c, 2, row, 1 - c).start()
    pl.loop(early, chunks)(lambda q: send_on(0, q))

    @pl.loop(1, span)
    def _(t):
        pl.loop(0, chunks)(lambda q: send_on(t, q))

    gate[...] = jax.nn.sigmoid(jnp.dot(normed[...], wg_ref[...], preferred_element_type=F32))
    left32[1 - y, c] = left[1 - y, c].astype(F32)
    for which in (y, 1 - y):
        left_copy(which, 1 - c, 0, row, c).wait_recv()
        left32[which, 1 - c] = left[which, 1 - c].astype(F32)

    def ret_copy(slot, pair):
        return pltpu.make_async_remote_copy(
            src_ref=stage.at[slot, pair], dst_ref=back.at[slot, pair],
            send_sem=ret_send.at[slot, pair], recv_sem=ret_recv.at[slot, pair],
            device_id={"row": across, "col": c}, device_id_type=MESH,
        )

    def sums(which, slot, pair, put):
        acc = [[None, None] for _ in range(rows)]
        for kc in range(2):
            wide = right[slot, kc, pl.ds(pair * 2 * cols, 2 * cols), :].astype(F32)
            for kt in range(0, cols, 8):
                r = [wide[j * cols + kt : j * cols + kt + 8] for j in range(2)]
                for i in range(rows):
                    l = left32[which, kc, i * cols + kt : i * cols + kt + 8, :]
                    for j in range(2):
                        term = l * r[j]
                        acc[i][j] = term if acc[i][j] is None else acc[i][j] + term
        for i in range(rows):
            for j in range(2):
                put(i, j, jnp.sum(acc[i][j], axis=0, keepdims=True))

    def place(i, j, slot, pair, side, value):
        comb[pl.ds(i * cols + (slot * 2 + side) * rows + pair * 2 + j, 1), :] = value

    @pl.loop(0, span)
    def _(t):
        zs = source(lax.rem(t + jnp.where((z >= low) & (z < low + span), span - 1, 0), span))
        slot = zs - low

        @pl.loop(0, pairs)
        def _(pair):
            for kc in range(2):
                @pl.when(jnp.logical_not(passes(zs)) & ((zs != z) | (c != kc)))
                def _(kc=kc):
                    for q in range(sub):
                        block(slot, kc, pair * sub + q, row).wait_recv()

            def put_stage(i, j, value):
                stage[slot, pair, j * rows + i : j * rows + i + 1, :] = value

            sums(1 - y, slot, pair, put_stage)
            sums(y, slot, pair, lambda i, j, value: place(i, j, slot, pair, y, value))
            ret_copy(slot, pair).start()

    @pl.loop(0, span)
    def _(t):
        slot = source(lax.rem(t + jnp.where((z >= low) & (z < low + span), span - 1, 0), span)) - low

        @pl.loop(0, pairs)
        def _(pair):
            ret_copy(slot, pair).wait_recv()
            for i in range(rows):
                for j in range(2):
                    got = back[slot, pair, j * rows + i : j * rows + i + 1, :]
                    place(i, j, slot, pair, 1 - y, got)

    loads[3].wait()
    tri = layer_norm(comb[...]).astype(BF16)
    update = jnp.dot(tri, wo_ref[...], preferred_element_type=F32) * gate[...]
    out_ref[...] = update.astype(BF16)

    for p in range(pairs):
        own_all(p, lambda copy: copy.wait_send())
    left_copy(y, c, 0, across, c).wait_send()
    left_copy(y, c, 1, row, 1 - c).wait_send()
    left_copy(1 - y, c, 2, row, 1 - c).wait_send()

    @pl.loop(0, span)
    def _(slot):
        @pl.when(passes(slot + low))
        def _():
            @pl.loop(0, chunks)
            def _(q):
                for kc in range(2):
                    block(slot, kc, q, row).wait_send()

        for pair in range(pairs):
            ret_copy(slot, pair).wait_send()


def per_device(n, pair_rep, proj_weight, gate_weight, out_weight):
    rows, cols, channels = pair_rep.shape
    hid = out_weight.shape[0]
    flat = rows * cols
    pairs = rows // 2
    sub = 1
    chunks = pairs * sub
    span = n // 4
    padded = -(-2 * rows // 8) * 8
    vmem = pl.BlockSpec(memory_space=pltpu.VMEM)
    dma = pltpu.SemaphoreType.DMA
    out = pl.pallas_call(
        functools.partial(kernel, n, rows, cols, pairs, sub),
        out_shape=pltpu.VMEM((flat, channels), BF16),
        in_specs=[pl.BlockSpec(memory_space=pl.ANY)] * 4,
        out_specs=vmem,
        scratch_shapes=[
            pltpu.VMEM((flat, channels), BF16),
            pltpu.VMEM((2, channels, 2 * hid), BF16),
            pltpu.VMEM((channels, channels), BF16),
            pltpu.VMEM((hid, channels), BF16),
            pltpu.VMEM((flat, channels), BF16),
            dma((4,)),
            dma((pairs,)),
            pltpu.VMEM((flat, hid), BF16),
            pltpu.VMEM((span, 2, flat, hid), BF16),
            pltpu.VMEM((2, 2, flat, hid), BF16),
            pltpu.VMEM((2, 2, flat, hid), F32),
            pltpu.VMEM((flat, hid), F32),
            pltpu.VMEM((flat, channels), F32),
            pltpu.VMEM((span, pairs, padded, hid), F32),
            pltpu.VMEM((span, pairs, padded, hid), F32),
            dma((3, chunks)),
            dma((span, 2, chunks)),
            dma((span, 2, chunks)),
            dma((3,)),
            dma((2, 2)),
            dma((span, pairs)),
            dma((span, pairs)),
        ],
        compiler_params=pltpu.CompilerParams(
            collective_id=0, has_side_effects=True, vmem_limit_bytes=60 * 1024 * 1024
        ),
    )(pair_rep.reshape(flat, channels), proj_weight, gate_weight, out_weight)
    return out.reshape(rows, cols, channels)


def solution(mesh):
    placed = (P(("groups", "row"), "col", None), P(), P(), P())
    return jax.shard_map(
        functools.partial(per_device, mesh.shape["row"]),
        mesh=mesh,
        in_specs=placed,
        out_specs=P(("groups", "row"), "col", None),
        check_vma=False,
    )
```
